256 devices in a mesh: row: 32 (over z, y_hi, core), col: 8 (over x, y_lo).
Axes of the slice: x: 4, y: 4 (y_hi: 2, y_lo: 2; y = y_hi * 2 + y_lo), z: 8, core: 2. Of those that a mesh axis runs over, the one named last changes fastest.
Arguments:
- velocity: float32 [3, 32, 1024, 1024], P(None, None, 'row', 'col'), may hold values from -6 to 6
- dy_op: bfloat16 [1024, 1024], replicated, may hold values from -0.1875 to 0.1875
- dz_op: bfloat16 [1024, 1024], replicated, may hold values from -0.1875 to 0.1875
- node_force: float32 [3, 2048], P(None, ('row', 'col')), may hold values from -6 to 6
- node_cell: int32 [3, 2048], P(None, ('row', 'col')), may hold values from 0 to 1023, as said below
Outputs:
- tendency: float32 [3, 32, 1024, 1024], P(None, None, 'row', 'col')
The draws below stay inside these ranges and needn't reach their ends.
Inputs may be any that keep to these rules, and one draw needn't show every extreme that they name: `node_cell`: the nodes of the block held by device (r, c) of the mesh have their z coordinate in the c-th of the 8 equal ranges of z; x lies below 32, y below 1024.
All inputs are finite; a program needn't handle non-finite values.
Results may differ from the reference program's by a relative error of at most 0.0029.
Values sent between devices are 32-bit elements; how exact they have to be, the bound alone decides.
A program may use at most 384 MiB of HBM per device.

```python
import jax
import jax.numpy as jnp
from jax import lax

NY = 1024
NZ = 1024
NODE_DEV = 8
NX = 32
NODES = 2048
N_ROW = 32
N_COL = 8


def draw_node_cell(key, part):
    keys = jax.random.split(key, 3)
    total = NODE_DEV * N_ROW * N_COL
    counter = jnp.arange(total, dtype=jnp.int32)
    block_id = counter // NODE_DEV
    slot_id = counter % NODE_DEV
    col_of = block_id % N_COL
    span = NZ // N_COL
    x_cells = jax.random.randint(keys[0], (total,), 0, NX)
    x_cells = jnp.where(slot_id == 0, 0, x_cells)
    y_cells = jax.random.randint(keys[1], (total,), 0, NY)
    z_cells = col_of * span + jax.random.randint(keys[2], (total,), 0, span)
    z_cells = jnp.where(slot_id == NODE_DEV - 1, col_of * span + span - 1, z_cells)
    return jnp.stack([x_cells, y_cells, z_cells]).astype(jnp.int32)


def shard_levels(rng, extent, cuts, low, top_value):
    gain, own = 1.0, jax.random.fold_in(rng, 6)
    for position, parts in cuts:
        heights = jnp.exp(jax.random.uniform(jax.random.fold_in(own, position), (parts,), jnp.float32, low / len(cuts), top_value / len(cuts)))
        gain = gain * jnp.repeat(heights, extent[position] // parts).reshape([-1 if axis == position else 1 for axis in range(len(extent))])
    return gain


def noise(rng, dims, width, reach, cuts=(), held_as=jnp.bfloat16):
    entries = jax.random.normal(rng, dims, jnp.float32) * width
    if len(cuts) > 0:
        entries = shard_levels(rng, dims, cuts, -0.22, 0.18) * entries
    return jnp.clip(entries, min=-reach, max=reach).astype(held_as)


def setup_inputs(seed: int = 0) -> dict:
    arg_keys = jax.random.split(jax.random.key(seed), 6)
    return {
        "velocity": noise(arg_keys[0], (3, NX, NY, NZ), 1.0, 6.0, ((2, 32), (3, 8)), jnp.float32),
        "dy_op": noise(arg_keys[1], (NY, NY), NY ** -0.5, 0.1875),
        "dz_op": noise(arg_keys[2], (NZ, NZ), NZ ** -0.5, 0.1875),
        "node_force": noise(arg_keys[3], (3, NODES), 1.0, 6.0, ((1, 256),), jnp.float32),
        "node_cell": draw_node_cell(jax.random.fold_in(arg_keys[5], 71), 0),
    }


def reference(velocity, dy_op, dz_op, node_force, node_cell):
    coarse = lax.optimization_barrier(velocity.astype(jnp.bfloat16)).astype(jnp.float32)
    dy_full = dy_op.astype(jnp.float32)
    full_z_derivative = dz_op.astype(jnp.float32)

    def one_plane(both_parts):
        exact_f, coarse_f = both_parts
        gradient_in_y = jnp.einsum('ab,cbz->caz', dy_full, coarse_f)
        gradient_in_z = jnp.einsum('cyb,ab->cya', coarse_f, full_z_derivative)
        return -(exact_f[1][None] * gradient_in_y + exact_f[2][None] * gradient_in_z)

    planes = lax.map(one_plane, (jnp.moveaxis(velocity, 1, 0), jnp.moveaxis(coarse, 1, 0)))
    tendency = jnp.moveaxis(planes, 0, 1)
    flat_index = ((node_cell[0] * NY + node_cell[1]) * NZ + node_cell[2]).astype(jnp.int32)
    summed = tendency.reshape(3, -1).at[:, flat_index].add(node_force)
    return summed.reshape(tendency.shape)
```

```python
import functools

import jax
import jax.numpy as jnp
from jax import lax
from jax.experimental import pallas as pl
from jax.experimental.pallas import tpu as pltpu
from jax.sharding import PartitionSpec as P

MESH = pl.DeviceIdType.MESH
F32 = jnp.float32
BF16 = jnp.bfloat16
COMPS = 3


def kernel(
    n_row, n_col,
    vel, dy_hbm, dz_hbm, force, cell,
    out,
    dy, dz, vw, y_in, z_in, y_out, z_out, y_back, z_back, node_tile, node_all, delta,
    load_sem, y_in_sem, z_in_sem, y_back_sem, z_back_sem, node_sem,
    y_in_send, z_in_send, y_back_send, z_back_send, node_send,
):
    r = lax.axis_index("row")
    c = lax.axis_index("col")
    ny, nz = vel.shape[2], vel.shape[3]
    planes = vel.shape[1] // n_col
    n_nodes = force.shape[1]

    barrier = pltpu.get_barrier_semaphore()

    @pl.loop(1, n_row)
    def _(s):
        pl.semaphore_signal(
            barrier, inc=1, device_id={"row": lax.rem(r + s, n_row)}, device_id_type=MESH
        )

    @pl.loop(1, n_col)
    def _(s):
        pl.semaphore_signal(
            barrier, inc=1, device_id={"col": lax.rem(c + s, n_col)}, device_id_type=MESH
        )

    load_dy = pltpu.make_async_copy(dy_hbm, dy, load_sem.at[0])
    load_dz = pltpu.make_async_copy(dz_hbm, dz, load_sem.at[1])
    load_vw = pltpu.make_async_copy(vel.at[pl.ds(1, 2)], vw, load_sem.at[2])

    group = (n_row * n_nodes) // 128
    per_tile = n_row // group
    lane = lax.broadcasted_iota(jnp.int32, (COMPS, 128), 1)
    base = lax.rem(r, per_tile) * n_nodes
    forces, cells = force[...], cell[...].astype(F32)
    spread_f = jnp.zeros((COMPS, 128), F32)
    spread_c = jnp.zeros((COMPS, 128), F32)
    for k in range(n_nodes):
        spread_f = jnp.where(lane == base + k, forces[:, k : k + 1], spread_f)
        spread_c = jnp.where(lane == base + k, cells[:, k : k + 1], spread_c)
    node_tile[...] = jnp.zeros_like(node_tile)
    node_tile[0:COMPS, :] = spread_f
    node_tile[4 : 4 + COMPS, :] = spread_c

    pl.semaphore_wait(barrier, n_row + n_col - 2)

    for k in range(COMPS):

        @pl.loop(1, n_row)
        def _(s):
            to = lax.rem(r + s, n_row)
            pltpu.make_async_remote_copy(
                src_ref=vel.at[k, to],
                dst_ref=y_in.at[k, pl.ds(pl.multiple_of(r * ny, ny), ny)],
                send_sem=y_in_send.at[k],
                recv_sem=y_in_sem.at[k],
                device_id={"row": to},
                device_id_type=MESH,
            ).start()

        @pl.loop(1, n_col)
        def _(s):
            to = lax.rem(c + s, n_col)
            pltpu.make_async_remote_copy(
                src_ref=vel.at[k, pl.ds(to * planes, planes)],
                dst_ref=z_in.at[k, c],
                send_sem=z_in_send.at[k],
                recv_sem=z_in_sem.at[k],
                device_id={"col": to},
                device_id_type=MESH,
            ).start()

        pltpu.make_async_copy(
            vel.at[k, r], y_in.at[k, pl.ds(pl.multiple_of(r * ny, ny), ny)], y_in_sem.at[k]
        ).start()
        pltpu.make_async_copy(
            vel.at[k, pl.ds(c * planes, planes)], z_in.at[k, c], z_in_sem.at[k]
        ).start()
        if k == 0:
            load_dy.start()
            load_dz.start()
            load_vw.start()

            @pl.loop(1, n_row)
            def _(s):
                pltpu.make_async_remote_copy(
                    src_ref=node_tile,
                    dst_ref=node_all.at[r],
                    send_sem=node_send,
                    recv_sem=node_sem,
                    device_id={"row": lax.rem(r + s, n_row)},
                    device_id_type=MESH,
                ).start()

            pltpu.make_async_copy(node_tile, node_all.at[r], node_sem).start()

    load_dy.wait()
    load_dz.wait()
    for k in range(COMPS):
        pltpu.make_async_copy(y_in.at[k], y_in.at[k], y_in_sem.at[k]).wait()
        lines = y_in[k].astype(BF16)
        rows = 256 if dy.shape[0] % 256 == 0 else dy.shape[0]
        for m in range(dy.shape[0] // rows):
            y_out[k, m * rows : (m + 1) * rows, :] = jnp.dot(
                dy[m * rows : (m + 1) * rows, :], lines, preferred_element_type=F32
            )

        @pl.loop(1, n_row)
        def _(s):
            to = lax.rem(r + s, n_row)
            pltpu.make_async_remote_copy(
                src_ref=y_out.at[k, pl.ds(pl.multiple_of(to * ny, ny), ny)],
                dst_ref=y_back.at[k, r],
                send_sem=y_back_send.at[k],
                recv_sem=y_back_sem.at[k],
                device_id={"row": to},
                device_id_type=MESH,
            ).start()

        pltpu.make_async_copy(
            y_out.at[k, pl.ds(pl.multiple_of(r * ny, ny), ny)], y_back.at[k, r], y_back_sem.at[k]
        ).start()

        pltpu.make_async_copy(z_in.at[k], z_in.at[k], z_in_sem.at[k]).wait()
        lines = jnp.concatenate(
            [z_in[k, j].reshape(planes * ny, nz) for j in range(n_col)], axis=1
        ).astype(BF16)
        for j in range(n_col):
            z_out[k, j] = lax.dot_general(
                lines, dz[j * nz : (j + 1) * nz, :], (((1,), (1,)), ((), ())),
                preferred_element_type=F32,
            ).reshape(planes, ny, nz)

        @pl.loop(1, n_col)
        def _(s):
            to = lax.rem(c + s, n_col)
            pltpu.make_async_remote_copy(
                src_ref=z_out.at[k, to],
                dst_ref=z_back.at[k, pl.ds(c * planes, planes)],
                send_sem=z_back_send.at[k],
                recv_sem=z_back_sem.at[k],
                device_id={"col": to},
                device_id_type=MESH,
            ).start()

        pltpu.make_async_copy(
            z_out.at[k, c], z_back.at[k, pl.ds(c * planes, planes)], z_back_sem.at[k]
        ).start()

    pltpu.make_async_copy(node_all, node_all, node_sem).wait()
    tiles = []
    for g in range(group):
        total = node_all[g * per_tile]
        for j in range(1, per_tile):
            total = total + node_all[g * per_tile + j]
        tiles.append(total)
    nodes = jnp.concatenate(tiles, axis=1)
    count = 128 * group
    first_y = (r * ny).astype(F32)
    first_z = (c * nz).astype(F32)
    local_y = nodes[5:6, :] - first_y
    owned = (local_y >= 0.0) & (local_y < float(ny))
    key = jnp.where(owned, nodes[4:5, :] * float(ny) + local_y, -1.0)
    key_z = nodes[6:7, :] - first_z
    z_pos = lax.broadcasted_iota(jnp.int32, (nz, count), 0).astype(F32)
    hot_z = jnp.where(z_pos == key_z, 1.0, 0.0).astype(BF16)
    high = nodes.astype(BF16).astype(F32)
    rest = nodes - high
    mid = rest.astype(BF16).astype(F32)
    low = rest - mid
    rows = vel.shape[1] * ny
    step = 256 if rows % 256 == 0 else rows

    @pl.loop(0, rows // step)
    def _(m):
        pos = (lax.broadcasted_iota(jnp.int32, (step, count), 0) + m * step).astype(F32)
        hit = pos == key
        for k in range(COMPS):
            total = jnp.zeros((step, nz), F32)
            for part in (high, mid, low):
                pushed = jnp.where(hit, part[k : k + 1, :], 0.0).astype(BF16)
                total = total + lax.dot_general(
                    pushed, hot_z, (((1,), (1,)), ((), ())), preferred_element_type=F32
                )
            delta[k, pl.ds(pl.multiple_of(m * step, step), step), :] = total

    load_vw.wait()
    for k in range(COMPS):
        pltpu.make_async_copy(y_back.at[k], y_back.at[k], y_back_sem.at[k]).wait()
        pltpu.make_async_copy(z_back.at[k], z_back.at[k], z_back_sem.at[k]).wait()
        out[k] = delta[k].reshape(out.shape[1:]) - (vw[0] * y_back[k] + vw[1] * z_back[k])

    for k in range(COMPS):
        y_sent = y_in.at[k, pl.ds(0, (n_row - 1) * ny)]
        z_sent = z_in.at[k, pl.ds(0, n_col - 1)]
        pltpu.make_async_copy(y_sent, y_sent, y_in_send.at[k]).wait()
        pltpu.make_async_copy(z_sent, z_sent, z_in_send.at[k]).wait()
        pltpu.make_async_copy(y_sent, y_sent, y_back_send.at[k]).wait()
        pltpu.make_async_copy(z_sent, z_sent, z_back_send.at[k]).wait()
    nodes_sent = node_all.at[pl.ds(0, n_row - 1)]
    pltpu.make_async_copy(nodes_sent, nodes_sent, node_send).wait()


def per_device(n_row, n_col, velocity, dy_op, dz_op, node_force, node_cell):
    _, n_x, ny, nz = velocity.shape
    planes = n_x // n_col
    dma = pltpu.SemaphoreType.DMA
    hbm = pl.BlockSpec(memory_space=pl.ANY)
    vmem = pl.BlockSpec(memory_space=pltpu.VMEM)
    return pl.pallas_call(
        functools.partial(kernel, n_row, n_col),
        out_shape=jax.ShapeDtypeStruct(velocity.shape, F32),
        in_specs=[hbm, hbm, hbm, vmem, vmem],
        out_specs=vmem,
        scratch_shapes=[
            pltpu.VMEM(dy_op.shape, BF16),
            pltpu.VMEM(dz_op.shape, BF16),
            pltpu.VMEM((2, n_x, ny, nz), F32),
            pltpu.VMEM((COMPS, n_row * ny, nz), F32),
            pltpu.VMEM((COMPS, n_col, planes, ny, nz), F32),
            pltpu.VMEM((COMPS, n_row * ny, nz), F32),
            pltpu.VMEM((COMPS, n_col, planes, ny, nz), F32),
            pltpu.VMEM((COMPS, n_x, ny, nz), F32),
            pltpu.VMEM((COMPS, n_x, ny, nz), F32),
            pltpu.VMEM((8, 128), F32),
            pltpu.VMEM((n_row, 8, 128), F32),
            pltpu.VMEM((COMPS, n_x * ny, nz), F32),
            dma((3,)), dma((COMPS,)), dma((COMPS,)), dma((COMPS,)), dma((COMPS,)), dma(()),
            dma((COMPS,)), dma((COMPS,)), dma((COMPS,)), dma((COMPS,)), dma(()),
        ],
        compiler_params=pltpu.CompilerParams(
            collective_id=0, has_side_effects=True, vmem_limit_bytes=48 * 1024 * 1024
        ),
    )(velocity, dy_op, dz_op, node_force, node_cell)


def solution(mesh):
    return jax.shard_map(
        functools.partial(per_device, mesh.shape["row"], mesh.shape["col"]),
        mesh=mesh,
        in_specs=(
            P(None, None, "row", "col"),
            P(),
            P(),
            P(None, ("row", "col")),
            P(None, ("row", "col")),
        ),
        out_specs=P(None, None, "row", "col"),
        check_vma=False,
    )
```

```python
import functools

import jax
import jax.numpy as jnp
from jax import lax
from jax.experimental import pallas as pl
from jax.experimental.pallas import tpu as pltpu
from jax.sharding import PartitionSpec as P

MESH = pl.DeviceIdType.MESH
F32 = jnp.float32
BF16 = jnp.bfloat16
COMPS = 3


def kernel(
    n_row, n_col,
    vel, dy_hbm, dz_hbm, force_hbm, cell_hbm,
    out,
    dy, dz, force, cell, vw, y_in, z_in, y_out, z_out, y_back, z_back, node_tile, node_all, delta,
    load_sem, y_in_sem, z_in_sem, y_back_sem, z_back_sem, node_sem,
    y_in_send, z_in_send, y_back_send, z_back_send, node_send,
):
    r = lax.axis_index("row")
    c = lax.axis_index("col")
    ny, nz = vel.shape[2], vel.shape[3]
    planes = vel.shape[1] // n_col
    n_nodes = force_hbm.shape[1]

    barrier = pltpu.get_barrier_semaphore()

    @pl.loop(1, n_row)
    def _(s):
        pl.semaphore_signal(
            barrier, inc=1, device_id={"row": lax.rem(r + s, n_row)}, device_id_type=MESH
        )

    @pl.loop(1, n_col)
    def _(s):
        pl.semaphore_signal(
            barrier, inc=1, device_id={"col": lax.rem(c + s, n_col)}, device_id_type=MESH
        )

    load_dy = pltpu.make_async_copy(dy_hbm, dy, load_sem.at[0])
    load_dz = pltpu.make_async_copy(dz_hbm, dz, load_sem.at[1])
    load_vw = pltpu.make_async_copy(vel.at[pl.ds(1, 2)], vw, load_sem.at[2])
    load_force = pltpu.make_async_copy(force_hbm, force, load_sem.at[3])
    load_cell = pltpu.make_async_copy(cell_hbm, cell, load_sem.at[4])
    load_force.start()
    load_cell.start()

    group = (n_row * n_nodes) // 128
    per_tile = n_row // group
    lane = lax.broadcasted_iota(jnp.int32, (COMPS, 128), 1)
    base = lax.rem(r, per_tile) * n_nodes
    load_force.wait()
    load_cell.wait()
    forces, cells = force[...], cell[...].astype(F32)
    spread_f = jnp.zeros((COMPS, 128), F32)
    spread_c = jnp.zeros((COMPS, 128), F32)
    for k in range(n_nodes):
        spread_f = jnp.where(lane == base + k, forces[:, k : k + 1], spread_f)
        spread_c = jnp.where(lane == base + k, cells[:, k : k + 1], spread_c)
    node_tile[...] = jnp.zeros_like(node_tile)
    node_tile[0:COMPS, :] = spread_f
    node_tile[4 : 4 + COMPS, :] = spread_c

    pl.semaphore_wait(barrier, n_row + n_col - 2)

    for k in range(COMPS):

        @pl.loop(1, n_row)
        def _(s):
            to = lax.rem(r + s, n_row)
            pltpu.make_async_remote_copy(
                src_ref=vel.at[k, to],
                dst_ref=y_in.at[k, pl.ds(pl.multiple_of(r * ny, ny), ny)],
                send_sem=y_in_send.at[k],
                recv_sem=y_in_sem.at[k],
                device_id={"row": to},
                device_id_type=MESH,
            ).start()

        @pl.loop(1, n_col)
        def _(s):
            to = lax.rem(c + s, n_col)
            pltpu.make_async_remote_copy(
                src_ref=vel.at[k, pl.ds(to * planes, planes)],
                dst_ref=z_in.at[k, c],
                send_sem=z_in_send.at[k],
                recv_sem=z_in_sem.at[k],
                device_id={"col": to},
                device_id_type=MESH,
            ).start()

        pltpu.make_async_copy(
            vel.at[k, r], y_in.at[k, pl.ds(pl.multiple_of(r * ny, ny), ny)], y_in_sem.at[k]
        ).start()
        pltpu.make_async_copy(
            vel.at[k, pl.ds(c * planes, planes)], z_in.at[k, c], z_in_sem.at[k]
        ).start()
        if k == 0:
            load_dy.start()
            load_dz.start()
            load_vw.start()

            @pl.loop(1, n_row)
            def _(s):
                pltpu.make_async_remote_copy(
                    src_ref=node_tile,
                    dst_ref=node_all.at[r],
                    send_sem=node_send,
                    recv_sem=node_sem,
                    device_id={"row": lax.rem(r + s, n_row)},
                    device_id_type=MESH,
                ).start()

            pltpu.make_async_copy(node_tile, node_all.at[r], node_sem).start()

    load_dy.wait()
    load_dz.wait()
    for k in range(COMPS):
        pltpu.make_async_copy(y_in.at[k], y_in.at[k], y_in_sem.at[k]).wait()
        lines = y_in[k].astype(BF16)
        rows = 256 if dy.shape[0] % 256 == 0 else dy.shape[0]
        for m in range(dy.shape[0] // rows):
            y_out[k, m * rows : (m + 1) * rows, :] = jnp.dot(
                dy[m * rows : (m + 1) * rows, :], lines, preferred_element_type=F32
            )

        @pl.loop(1, n_row)
        def _(s):
            to = lax.rem(r + s, n_row)
            pltpu.make_async_remote_copy(
                src_ref=y_out.at[k, pl.ds(pl.multiple_of(to * ny, ny), ny)],
                dst_ref=y_back.at[k, r],
                send_sem=y_back_send.at[k],
                recv_sem=y_back_sem.at[k],
                device_id={"row": to},
                device_id_type=MESH,
            ).start()

        pltpu.make_async_copy(
            y_out.at[k, pl.ds(pl.multiple_of(r * ny, ny), ny)], y_back.at[k, r], y_back_sem.at[k]
        ).start()

        pltpu.make_async_copy(z_in.at[k], z_in.at[k], z_in_sem.at[k]).wait()
        lines = jnp.concatenate(
            [z_in[k, j].reshape(planes * ny, nz) for j in range(n_col)], axis=1
        ).astype(BF16)
        for j in range(n_col):
            z_out[k, j] = lax.dot_general(
                lines, dz[j * nz : (j + 1) * nz, :], (((1,), (1,)), ((), ())),
                preferred_element_type=F32,
            ).reshape(planes, ny, nz)

        @pl.loop(1, n_col)
        def _(s):
            to = lax.rem(c + s, n_col)
            pltpu.make_async_remote_copy(
                src_ref=z_out.at[k, to],
                dst_ref=z_back.at[k, pl.ds(c * planes, planes)],
                send_sem=z_back_send.at[k],
                recv_sem=z_back_sem.at[k],
                device_id={"col": to},
                device_id_type=MESH,
            ).start()

        pltpu.make_async_copy(
            z_out.at[k, c], z_back.at[k, pl.ds(c * planes, planes)], z_back_sem.at[k]
        ).start()

    pltpu.make_async_copy(node_all, node_all, node_sem).wait()
    tiles = []
    for g in range(group):
        total = node_all[g * per_tile]
        for j in range(1, per_tile):
            total = total + node_all[g * per_tile + j]
        tiles.append(total)
    nodes = jnp.concatenate(tiles, axis=1)
    count = 128 * group
    first_y = (r * ny).astype(F32)
    first_z = (c * nz).astype(F32)
    local_y = nodes[5:6, :] - first_y
    owned = (local_y >= 0.0) & (local_y < float(ny))
    key = jnp.where(owned, nodes[4:5, :] * float(ny) + local_y, -1.0)
    key_z = nodes[6:7, :] - first_z
    z_pos = lax.broadcasted_iota(jnp.int32, (nz, count), 0).astype(F32)
    hot_z = jnp.where(z_pos == key_z, 1.0, 0.0).astype(BF16)
    high = nodes.astype(BF16).astype(F32)
    rest = nodes - high
    mid = rest.astype(BF16).astype(F32)
    low = rest - mid
    rows = vel.shape[1] * ny
    step = 256 if rows % 256 == 0 else rows

    @pl.loop(0, rows // step)
    def _(m):
        pos = (lax.broadcasted_iota(jnp.int32, (step, count), 0) + m * step).astype(F32)
        hit = pos == key
        for k in range(COMPS):
            total = jnp.zeros((step, nz), F32)
            for part in (high, mid, low):
                pushed = jnp.where(hit, part[k : k + 1, :], 0.0).astype(BF16)
                total = total + lax.dot_general(
                    pushed, hot_z, (((1,), (1,)), ((), ())), preferred_element_type=F32
                )
            delta[k, pl.ds(pl.multiple_of(m * step, step), step), :] = total

    load_vw.wait()
    for k in range(COMPS):
        pltpu.make_async_copy(y_back.at[k], y_back.at[k], y_back_sem.at[k]).wait()
        pltpu.make_async_copy(z_back.at[k], z_back.at[k], z_back_sem.at[k]).wait()
        out[k] = delta[k].reshape(out.shape[1:]) - (vw[0] * y_back[k] + vw[1] * z_back[k])

    for k in range(COMPS):
        y_sent = y_in.at[k, pl.ds(0, (n_row - 1) * ny)]
        z_sent = z_in.at[k, pl.ds(0, n_col - 1)]
        pltpu.make_async_copy(y_sent, y_sent, y_in_send.at[k]).wait()
        pltpu.make_async_copy(z_sent, z_sent, z_in_send.at[k]).wait()
        pltpu.make_async_copy(y_sent, y_sent, y_back_send.at[k]).wait()
        pltpu.make_async_copy(z_sent, z_sent, z_back_send.at[k]).wait()
    nodes_sent = node_all.at[pl.ds(0, n_row - 1)]
    pltpu.make_async_copy(nodes_sent, nodes_sent, node_send).wait()


def per_device(n_row, n_col, velocity, dy_op, dz_op, node_force, node_cell):
    _, n_x, ny, nz = velocity.shape
    planes = n_x // n_col
    dma = pltpu.SemaphoreType.DMA
    hbm = pl.BlockSpec(memory_space=pltpu.HBM)
    vmem = pl.BlockSpec(memory_space=pltpu.VMEM)
    return pl.pallas_call(
        functools.partial(kernel, n_row, n_col),
        out_shape=jax.ShapeDtypeStruct(velocity.shape, F32),
        in_specs=[hbm] * 5,
        out_specs=vmem,
        scratch_shapes=[
            pltpu.VMEM(dy_op.shape, BF16),
            pltpu.VMEM(dz_op.shape, BF16),
            pltpu.VMEM(node_force.shape, F32),
            pltpu.VMEM(node_cell.shape, jnp.int32),
            pltpu.VMEM((2, n_x, ny, nz), F32),
            pltpu.VMEM((COMPS, n_row * ny, nz), F32),
            pltpu.VMEM((COMPS, n_col, planes, ny, nz), F32),
            pltpu.VMEM((COMPS, n_row * ny, nz), F32),
            pltpu.VMEM((COMPS, n_col, planes, ny, nz), F32),
            pltpu.VMEM((COMPS, n_x, ny, nz), F32),
            pltpu.VMEM((COMPS, n_x, ny, nz), F32),
            pltpu.VMEM((8, 128), F32),
            pltpu.VMEM((n_row, 8, 128), F32),
            pltpu.VMEM((COMPS, n_x * ny, nz), F32),
            dma((5,)), dma((COMPS,)), dma((COMPS,)), dma((COMPS,)), dma((COMPS,)), dma(()),
            dma((COMPS,)), dma((COMPS,)), dma((COMPS,)), dma((COMPS,)), dma(()),
        ],
        compiler_params=pltpu.CompilerParams(
            collective_id=0, has_side_effects=True, vmem_limit_bytes=56 * 1024 * 1024
        ),
    )(velocity, dy_op, dz_op, node_force, node_cell)


def solution(mesh):
    return jax.shard_map(
        functools.partial(per_device, mesh.shape["row"], mesh.shape["col"]),
        mesh=mesh,
        in_specs=(
            P(None, None, "row", "col"),
            P(),
            P(),
            P(None, ("row", "col")),
            P(None, ("row", "col")),
        ),
        out_specs=P(None, None, "row", "col"),
        check_vma=False,
    )
```

```python
import functools

import jax
import jax.numpy as jnp
from jax import lax
from jax.experimental import pallas as pl
from jax.experimental.pallas import tpu as pltpu
from jax.sharding import PartitionSpec as P

MESH = pl.DeviceIdType.MESH
F32 = jnp.float32
BF16 = jnp.bfloat16
COMPS = 3
GROUP = 4


def wait_for(ref, sem):
    pltpu.make_async_copy(ref, ref, sem).wait()


def kernel(
    n_row, n_col,
    vel, dy_hbm, dz_hbm, force_hbm, cell_hbm,
    out,
    dy, dz, force, cell, vw,
    by_z, y_in, y_out, by_group, y_back, z_in, z_out, z_back,
    node_tile, node_z, node_all, delta,
    load_sem, by_z_sem, y_in_sem, by_group_sem, y_back_sem, z_in_sem, z_back_sem, node_sem,
    by_z_send, y_in_send, by_group_send, y_back_send, z_in_send, z_back_send, node_send,
):
    n_z = n_row // GROUP
    r = lax.axis_index("row")
    c = lax.axis_index("col")
    z, q = r // GROUP, r % GROUP
    ny, nz = vel.shape[2], vel.shape[3]
    planes = vel.shape[1] // n_col
    n_nodes = force_hbm.shape[1]
    z_offsets = sorted(range(1, n_z), key=lambda d: -min(d, n_z - d))

    def along_z(d):
        return (z + d) % n_z

    def in_group(d):
        return (q + d) % GROUP

    def along_col(d):
        return (c + d) % n_col

    def send(src, dst, send_sem, recv_sem, **to):
        pltpu.make_async_remote_copy(
            src_ref=src, dst_ref=dst, send_sem=send_sem, recv_sem=recv_sem,
            device_id=to, device_id_type=MESH,
        ).start()

    barrier = pltpu.get_barrier_semaphore()
    for d in z_offsets:
        pl.semaphore_signal(
            barrier, inc=1, device_id={"row": along_z(d) * GROUP + q}, device_id_type=MESH
        )
    for d in range(1, n_col):
        pl.semaphore_signal(barrier, inc=1, device_id={"col": along_col(d)}, device_id_type=MESH)
    for d in range(1, GROUP):
        pl.semaphore_signal(
            barrier, inc=1, device_id={"row": z * GROUP + in_group(d)}, device_id_type=MESH
        )

    load_dy = pltpu.make_async_copy(dy_hbm, dy, load_sem.at[0])
    load_dz = pltpu.make_async_copy(dz_hbm, dz, load_sem.at[1])
    load_vw = pltpu.make_async_copy(vel.at[pl.ds(1, 2)], vw, load_sem.at[2])
    load_force = pltpu.make_async_copy(force_hbm, force, load_sem.at[3])
    load_cell = pltpu.make_async_copy(cell_hbm, cell, load_sem.at[4])
    load_force.start()
    load_cell.start()
    for k in range(COMPS):
        pltpu.make_async_copy(
            vel.at[k, pl.ds(z * GROUP, GROUP)], by_z.at[k, z], by_z_sem.at[k]
        ).start()
        pltpu.make_async_copy(
            vel.at[k, pl.ds(c * planes, planes)], z_in.at[k, c], z_in_sem.at[k]
        ).start()
    load_dz.start()
    load_dy.start()
    load_vw.start()

    pl.semaphore_wait(barrier, n_z + n_col + GROUP - 3)

    def z_forward(k):
        for d in z_offsets:
            to = along_z(d)
            send(
                vel.at[k, pl.ds(to * GROUP, GROUP)], by_z.at[k, z],
                by_z_send.at[k], by_z_sem.at[k], row=to * GROUP + q,
            )

    def group_forward(k):
        wait_for(by_z.at[k], by_z_sem.at[k])
        for d in range(1, GROUP):
            to = in_group(d)
            send(
                by_z.at[k, :, to], y_in.at[k, :, q],
                y_in_send.at[k], y_in_sem.at[k], row=z * GROUP + to,
            )
        pltpu.make_async_copy(by_z.at[k, :, q], y_in.at[k, :, q], y_in_sem.at[k]).start()

    def y_gradient(k):
        wait_for(y_in.at[k], y_in_sem.at[k])
        lines = y_in[k].reshape(n_row * ny, nz).astype(BF16)
        rows = 2 * GROUP * ny
        for m in range(n_z // 2):
            y_out[k, 2 * m : 2 * m + 2] = jnp.dot(
                dy[m * rows : (m + 1) * rows, :], lines, preferred_element_type=F32
            ).reshape(2, GROUP, ny, nz)
        for d in range(1, GROUP):
            to = in_group(d)
            send(
                y_out.at[k, :, to], by_group.at[k, :, q],
                by_group_send.at[k], by_group_sem.at[k], row=z * GROUP + to,
            )
        pltpu.make_async_copy(
            y_out.at[k, :, q], by_group.at[k, :, q], by_group_sem.at[k]
        ).start()

    def z_return(k):
        wait_for(by_group.at[k], by_group_sem.at[k])
        for d in z_offsets:
            to = along_z(d)
            send(
                by_group.at[k, to], y_back.at[k, pl.ds(z * GROUP, GROUP)],
                y_back_send.at[k], y_back_sem.at[k], row=to * GROUP + q,
            )
        pltpu.make_async_copy(
            by_group.at[k, z], y_back.at[k, pl.ds(z * GROUP, GROUP)], y_back_sem.at[k]
        ).start()

    def col_forward(k):
        for d in range(1, n_col):
            to = along_col(d)
            send(
                vel.at[k, pl.ds(to * planes, planes)], z_in.at[k, c],
                z_in_send.at[k], z_in_sem.at[k], col=to,
            )

    def z_gradient(k):
        wait_for(z_in.at[k], z_in_sem.at[k])
        lines = jnp.concatenate(
            [z_in[k, j].reshape(planes * ny, nz) for j in range(n_col)], axis=1
        ).astype(BF16)
        for j in range(n_col):
            z_out[k, j] = lax.dot_general(
                lines, dz[j * nz : (j + 1) * nz, :], (((1,), (1,)), ((), ())),
                preferred_element_type=F32,
            ).reshape(planes, ny, nz)

    def col_return(k):
        for d in range(1, n_col):
            to = along_col(d)
            send(
                z_out.at[k, to], z_back.at[k, pl.ds(c * planes, planes)],
                z_back_send.at[k], z_back_sem.at[k], col=to,
            )
        pltpu.make_async_copy(
            z_out.at[k, c], z_back.at[k, pl.ds(c * planes, planes)], z_back_sem.at[k]
        ).start()

    for k in range(COMPS):
        z_forward(k)
    for k in range(COMPS):
        col_forward(k)

    group = (n_row * n_nodes) // 128
    per_tile = n_row // group
    lane = lax.broadcasted_iota(jnp.int32, (COMPS, 128), 1)
    base = (r % per_tile) * n_nodes
    load_force.wait()
    load_cell.wait()
    forces, cells = force[...], cell[...].astype(F32)
    spread_f = jnp.zeros((COMPS, 128), F32)
    spread_c = jnp.zeros((COMPS, 128), F32)
    for k in range(n_nodes):
        spread_f = jnp.where(lane == base + k, forces[:, k : k + 1], spread_f)
        spread_c = jnp.where(lane == base + k, cells[:, k : k + 1], spread_c)
    node_tile[...] = jnp.zeros_like(node_tile)
    node_tile[0:COMPS, :] = spread_f
    node_tile[4 : 4 + COMPS, :] = spread_c
    for d in z_offsets:
        send(
            node_tile, node_z.at[z], node_send.at[0], node_sem.at[0],
            row=along_z(d) * GROUP + q,
        )
    pltpu.make_async_copy(node_tile, node_z.at[z], node_sem.at[0]).start()

    load_dz.wait()
    load_dy.wait()
    group_forward(0)
    z_gradient(0)
    y_gradient(0)
    z_gradient(1)
    group_forward(1)
    z_return(0)
    z_gradient(2)
    y_gradient(1)
    group_forward(2)
    z_return(1)

    wait_for(node_z, node_sem.at[0])
    for d in range(1, GROUP):
        send(
            node_z, node_all.at[q], node_send.at[1], node_sem.at[1],
            row=z * GROUP + in_group(d),
        )
    pltpu.make_async_copy(node_z, node_all.at[q], node_sem.at[1]).start()

    y_gradient(2)
    for k in range(COMPS):
        col_return(k)
    z_return(2)

    wait_for(node_all, node_sem.at[1])
    tiles = []
    z_per_tile = per_tile // GROUP
    for g in range(group):
        total = node_all[0, g * z_per_tile]
        for j in range(GROUP):
            for i in range(z_per_tile):
                if i or j:
                    total = total + node_all[j, g * z_per_tile + i]
        tiles.append(total)
    nodes = jnp.concatenate(tiles, axis=1)
    count = 128 * group
    first_y = (r * ny).astype(F32)
    first_z = (c * nz).astype(F32)
    local_y = nodes[5:6, :] - first_y
    owned = (local_y >= 0.0) & (local_y < float(ny))
    key = jnp.where(owned, nodes[4:5, :] * float(ny) + local_y, -1.0)
    key_z = nodes[6:7, :] - first_z
    z_pos = lax.broadcasted_iota(jnp.int32, (nz, count), 0).astype(F32)
    hot_z = jnp.where(z_pos == key_z, 1.0, 0.0).astype(BF16)
    high = nodes.astype(BF16).astype(F32)
    rest = nodes - high
    mid = rest.astype(BF16).astype(F32)
    low = rest - mid
    rows = vel.shape[1] * ny
    step = 256 if rows % 256 == 0 else rows

    @pl.loop(0, rows // step)
    def _(m):
        pos = (lax.broadcasted_iota(jnp.int32, (step, count), 0) + m * step).astype(F32)
        hit = pos == key
        for k in range(COMPS):
            total = jnp.zeros((step, nz), F32)
            for part in (high, mid, low):
                pushed = jnp.where(hit, part[k : k + 1, :], 0.0).astype(BF16)
                total = total + lax.dot_general(
                    pushed, hot_z, (((1,), (1,)), ((), ())), preferred_element_type=F32
                )
            delta[k, pl.ds(pl.multiple_of(m * step, step), step), :] = total

    load_vw.wait()
    for k in range(COMPS):
        wait_for(z_back.at[k], z_back_sem.at[k])
        wait_for(y_back.at[k], y_back_sem.at[k])
        out[k] = delta[k].reshape(out.shape[1:]) - (vw[0] * y_back[k] + vw[1] * z_back[k])

    for k in range(COMPS):
        z_sent = by_z.at[k, pl.ds(0, n_z - 1)]
        group_sent = by_z.at[k, :, pl.ds(0, GROUP - 1)]
        col_sent = z_in.at[k, pl.ds(0, n_col - 1)]
        wait_for(z_sent, by_z_send.at[k])
        wait_for(group_sent, y_in_send.at[k])
        wait_for(group_sent, by_group_send.at[k])
        wait_for(z_sent, y_back_send.at[k])
        wait_for(col_sent, z_in_send.at[k])
        wait_for(col_sent, z_back_send.at[k])
    wait_for(node_z.at[pl.ds(0, n_z - 1)], node_send.at[0])
    wait_for(node_all.at[pl.ds(0, GROUP - 1)], node_send.at[1])


def per_device(n_row, n_col, velocity, dy_op, dz_op, node_force, node_cell):
    _, n_x, ny, nz = velocity.shape
    planes = n_x // n_col
    n_z = n_row // GROUP
    dma = pltpu.SemaphoreType.DMA
    hbm = pl.BlockSpec(memory_space=pltpu.HBM)
    vmem = pl.BlockSpec(memory_space=pltpu.VMEM)
    lines = pltpu.VMEM((COMPS, n_z, GROUP, ny, nz), F32)
    owned = pltpu.VMEM((COMPS, n_x, ny, nz), F32)
    col_lines = pltpu.VMEM((COMPS, n_col, planes, ny, nz), F32)
    return pl.pallas_call(
        functools.partial(kernel, n_row, n_col),
        out_shape=jax.ShapeDtypeStruct(velocity.shape, F32),
        in_specs=[hbm] * 5,
        out_specs=vmem,
        scratch_shapes=[
            pltpu.VMEM(dy_op.shape, BF16),
            pltpu.VMEM(dz_op.shape, BF16),
            pltpu.VMEM(node_force.shape, F32),
            pltpu.VMEM(node_cell.shape, jnp.int32),
            pltpu.VMEM((2, n_x, ny, nz), F32),
            lines, lines, lines, lines, owned, col_lines, col_lines, owned,
            pltpu.VMEM((8, 128), F32),
            pltpu.VMEM((n_z, 8, 128), F32),
            pltpu.VMEM((GROUP, n_z, 8, 128), F32),
            pltpu.VMEM((COMPS, n_x * ny, nz), F32),
            dma((5,)), *[dma((COMPS,))] * 6, dma((2,)),
            *[dma((COMPS,))] * 6, dma((2,)),
        ],
        compiler_params=pltpu.CompilerParams(
            collective_id=0, has_side_effects=True, vmem_limit_bytes=40 * 1024 * 1024
        ),
    )(*(
        pltpu.with_memory_space_constraint(x, pltpu.HBM)
        for x in (velocity, dy_op, dz_op, node_force, node_cell)
    ))


def solution(mesh):
    return jax.shard_map(
        functools.partial(per_device, mesh.shape["row"], mesh.shape["col"]),
        mesh=mesh,
        in_specs=(
            P(None, None, "row", "col"),
            P(),
            P(),
            P(None, ("row", "col")),
            P(None, ("row", "col")),
        ),
        out_specs=P(None, None, "row", "col"),
        check_vma=False,
    )
```

```python
import functools

import jax
import jax.numpy as jnp
from jax import lax
from jax.experimental import pallas as pl
from jax.experimental.pallas import tpu as pltpu
from jax.sharding import PartitionSpec as P

MESH = pl.DeviceIdType.MESH
F32 = jnp.float32
BF16 = jnp.bfloat16
COMPS = 3
GROUP = 4
RETURN_ORDER = (0, 1, 2, 4, 3, 7, 6, 5)


def return_order(n_z):
    return [p for p in RETURN_ORDER if p < n_z] + list(range(len(RETURN_ORDER), n_z))


def kernel(
    n_row, n_col,
    vel, dy_hbm, dz_hbm, force_hbm, cell_hbm,
    out,
    dy, dz, force, cell, vw, y_in, z_in, y_out, z_out, y_back, z_back, node_tile, node_all, delta,
    load_sem, y_in_sem, z_in_sem, y_back_sem, z_back_sem, node_sem,
    y_in_send, z_in_send, y_back_send, z_back_send, node_send,
):
    r = lax.axis_index("row")
    c = lax.axis_index("col")
    ny, nz = vel.shape[2], vel.shape[3]
    planes = vel.shape[1] // n_col
    n_nodes = force_hbm.shape[1]

    barrier = pltpu.get_barrier_semaphore()

    @pl.loop(1, n_row)
    def _(s):
        pl.semaphore_signal(
            barrier, inc=1, device_id={"row": lax.rem(r + s, n_row)}, device_id_type=MESH
        )

    @pl.loop(1, n_col)
    def _(s):
        pl.semaphore_signal(
            barrier, inc=1, device_id={"col": lax.rem(c + s, n_col)}, device_id_type=MESH
        )

    load_dy = pltpu.make_async_copy(dy_hbm, dy, load_sem.at[0])
    load_dz = pltpu.make_async_copy(dz_hbm, dz, load_sem.at[1])
    load_vw = pltpu.make_async_copy(vel.at[pl.ds(1, 2)], vw, load_sem.at[2])
    load_force = pltpu.make_async_copy(force_hbm, force, load_sem.at[3])
    load_cell = pltpu.make_async_copy(cell_hbm, cell, load_sem.at[4])
    load_force.start()
    load_cell.start()

    group = (n_row * n_nodes) // 128
    per_tile = n_row // group
    lane = lax.broadcasted_iota(jnp.int32, (COMPS, 128), 1)
    base = lax.rem(r, per_tile) * n_nodes
    load_force.wait()
    load_cell.wait()
    forces, cells = force[...], cell[...].astype(F32)
    spread_f = jnp.zeros((COMPS, 128), F32)
    spread_c = jnp.zeros((COMPS, 128), F32)
    for k in range(n_nodes):
        spread_f = jnp.where(lane == base + k, forces[:, k : k + 1], spread_f)
        spread_c = jnp.where(lane == base + k, cells[:, k : k + 1], spread_c)
    node_tile[...] = jnp.zeros_like(node_tile)
    node_tile[0:COMPS, :] = spread_f
    node_tile[4 : 4 + COMPS, :] = spread_c

    pl.semaphore_wait(barrier, n_row + n_col - 2)

    for k in range(COMPS):

        @pl.loop(1, n_row)
        def _(s):
            to = lax.rem(r + s, n_row)
            pltpu.make_async_remote_copy(
                src_ref=vel.at[k, to],
                dst_ref=y_in.at[k, pl.ds(pl.multiple_of(r * ny, ny), ny)],
                send_sem=y_in_send.at[k],
                recv_sem=y_in_sem.at[k],
                device_id={"row": to},
                device_id_type=MESH,
            ).start()

        @pl.loop(1, n_col)
        def _(s):
            to = lax.rem(c + s, n_col)
            pltpu.make_async_remote_copy(
                src_ref=vel.at[k, pl.ds(to * planes, planes)],
                dst_ref=z_in.at[k, c],
                send_sem=z_in_send.at[k],
                recv_sem=z_in_sem.at[k],
                device_id={"col": to},
                device_id_type=MESH,
            ).start()

        pltpu.make_async_copy(
            vel.at[k, r], y_in.at[k, pl.ds(pl.multiple_of(r * ny, ny), ny)], y_in_sem.at[k]
        ).start()
        pltpu.make_async_copy(
            vel.at[k, pl.ds(c * planes, planes)], z_in.at[k, c], z_in_sem.at[k]
        ).start()
        if k == 0:
            load_dy.start()
            load_dz.start()
            load_vw.start()

            @pl.loop(1, n_row)
            def _(s):
                pltpu.make_async_remote_copy(
                    src_ref=node_tile,
                    dst_ref=node_all.at[r],
                    send_sem=node_send,
                    recv_sem=node_sem,
                    device_id={"row": lax.rem(r + s, n_row)},
                    device_id_type=MESH,
                ).start()

            pltpu.make_async_copy(node_tile, node_all.at[r], node_sem).start()

    load_dy.wait()
    load_dz.wait()
    for k in range(COMPS):
        pltpu.make_async_copy(y_in.at[k], y_in.at[k], y_in_sem.at[k]).wait()
        lines = y_in[k].astype(BF16)
        rows = 256 if dy.shape[0] % 256 == 0 else dy.shape[0]
        for m in range(dy.shape[0] // rows):
            y_out[k, m * rows : (m + 1) * rows, :] = jnp.dot(
                dy[m * rows : (m + 1) * rows, :], lines, preferred_element_type=F32
            )

        def y_return(to):
            pltpu.make_async_remote_copy(
                src_ref=y_out.at[k, pl.ds(pl.multiple_of(to * ny, ny), ny)],
                dst_ref=y_back.at[k, r],
                send_sem=y_back_send.at[k],
                recv_sem=y_back_sem.at[k],
                device_id={"row": to},
                device_id_type=MESH,
            ).start()

        for to_z in return_order(n_row // GROUP):

            @pl.loop(0, GROUP)
            def _(s):
                to = to_z * GROUP + lax.rem(r + s, GROUP)

                @pl.when(to != r)
                def _():
                    y_return(to)

        pltpu.make_async_copy(
            y_out.at[k, pl.ds(pl.multiple_of(r * ny, ny), ny)], y_back.at[k, r], y_back_sem.at[k]
        ).start()

        pltpu.make_async_copy(z_in.at[k], z_in.at[k], z_in_sem.at[k]).wait()
        lines = jnp.concatenate(
            [z_in[k, j].reshape(planes * ny, nz) for j in range(n_col)], axis=1
        ).astype(BF16)
        for j in range(n_col):
            z_out[k, j] = lax.dot_general(
                lines, dz[j * nz : (j + 1) * nz, :], (((1,), (1,)), ((), ())),
                preferred_element_type=F32,
            ).reshape(planes, ny, nz)

        @pl.loop(1, n_col)
        def _(s):
            to = lax.rem(c + s, n_col)
            pltpu.make_async_remote_copy(
                src_ref=z_out.at[k, to],
                dst_ref=z_back.at[k, pl.ds(c * planes, planes)],
                send_sem=z_back_send.at[k],
                recv_sem=z_back_sem.at[k],
                device_id={"col": to},
                device_id_type=MESH,
            ).start()

        pltpu.make_async_copy(
            z_out.at[k, c], z_back.at[k, pl.ds(c * planes, planes)], z_back_sem.at[k]
        ).start()

    pltpu.make_async_copy(node_all, node_all, node_sem).wait()
    tiles = []
    for g in range(group):
        total = node_all[g * per_tile]
        for j in range(1, per_tile):
            total = total + node_all[g * per_tile + j]
        tiles.append(total)
    nodes = jnp.concatenate(tiles, axis=1)
    count = 128 * group
    first_y = (r * ny).astype(F32)
    first_z = (c * nz).astype(F32)
    local_y = nodes[5:6, :] - first_y
    owned = (local_y >= 0.0) & (local_y < float(ny))
    key = jnp.where(owned, nodes[4:5, :] * float(ny) + local_y, -1.0)
    key_z = nodes[6:7, :] - first_z
    z_pos = lax.broadcasted_iota(jnp.int32, (nz, count), 0).astype(F32)
    hot_z = jnp.where(z_pos == key_z, 1.0, 0.0).astype(BF16)
    high = nodes.astype(BF16).astype(F32)
    rest = nodes - high
    mid = rest.astype(BF16).astype(F32)
    low = rest - mid
    rows = vel.shape[1] * ny
    step = 256 if rows % 256 == 0 else rows

    @pl.loop(0, rows // step)
    def _(m):
        pos = (lax.broadcasted_iota(jnp.int32, (step, count), 0) + m * step).astype(F32)
        hit = pos == key
        for k in range(COMPS):
            total = jnp.zeros((step, nz), F32)
            for part in (high, mid, low):
                pushed = jnp.where(hit, part[k : k + 1, :], 0.0).astype(BF16)
                total = total + lax.dot_general(
                    pushed, hot_z, (((1,), (1,)), ((), ())), preferred_element_type=F32
                )
            delta[k, pl.ds(pl.multiple_of(m * step, step), step), :] = total

    load_vw.wait()
    for k in range(COMPS):
        pltpu.make_async_copy(y_back.at[k], y_back.at[k], y_back_sem.at[k]).wait()
        pltpu.make_async_copy(z_back.at[k], z_back.at[k], z_back_sem.at[k]).wait()
        out[k] = delta[k].reshape(out.shape[1:]) - (vw[0] * y_back[k] + vw[1] * z_back[k])

    for k in range(COMPS):
        y_sent = y_in.at[k, pl.ds(0, (n_row - 1) * ny)]
        z_sent = z_in.at[k, pl.ds(0, n_col - 1)]
        pltpu.make_async_copy(y_sent, y_sent, y_in_send.at[k]).wait()
        pltpu.make_async_copy(z_sent, z_sent, z_in_send.at[k]).wait()
        pltpu.make_async_copy(y_sent, y_sent, y_back_send.at[k]).wait()
        pltpu.make_async_copy(z_sent, z_sent, z_back_send.at[k]).wait()
    nodes_sent = node_all.at[pl.ds(0, n_row - 1)]
    pltpu.make_async_copy(nodes_sent, nodes_sent, node_send).wait()


def per_device(n_row, n_col, velocity, dy_op, dz_op, node_force, node_cell):
    _, n_x, ny, nz = velocity.shape
    planes = n_x // n_col
    dma = pltpu.SemaphoreType.DMA
    hbm = pl.BlockSpec(memory_space=pltpu.HBM)
    vmem = pl.BlockSpec(memory_space=pltpu.VMEM)
    return pl.pallas_call(
        functools.partial(kernel, n_row, n_col),
        out_shape=jax.ShapeDtypeStruct(velocity.shape, F32),
        in_specs=[hbm] * 5,
        out_specs=vmem,
        scratch_shapes=[
            pltpu.VMEM(dy_op.shape, BF16),
            pltpu.VMEM(dz_op.shape, BF16),
            pltpu.VMEM(node_force.shape, F32),
            pltpu.VMEM(node_cell.shape, jnp.int32),
            pltpu.VMEM((2, n_x, ny, nz), F32),
            pltpu.VMEM((COMPS, n_row * ny, nz), F32),
            pltpu.VMEM((COMPS, n_col, planes, ny, nz), F32),
            pltpu.VMEM((COMPS, n_row * ny, nz), F32),
            pltpu.VMEM((COMPS, n_col, planes, ny, nz), F32),
            pltpu.VMEM((COMPS, n_x, ny, nz), F32),
            pltpu.VMEM((COMPS, n_x, ny, nz), F32),
            pltpu.VMEM((8, 128), F32),
            pltpu.VMEM((n_row, 8, 128), F32),
            pltpu.VMEM((COMPS, n_x * ny, nz), F32),
            dma((5,)), dma((COMPS,)), dma((COMPS,)), dma((COMPS,)), dma((COMPS,)), dma(()),
            dma((COMPS,)), dma((COMPS,)), dma((COMPS,)), dma((COMPS,)), dma(()),
        ],
        compiler_params=pltpu.CompilerParams(
            collective_id=0, has_side_effects=True, vmem_limit_bytes=40 * 1024 * 1024
        ),
    )(*(
        pltpu.with_memory_space_constraint(x, pltpu.HBM)
        for x in (velocity, dy_op, dz_op, node_force, node_cell)
    ))


def solution(mesh):
    return jax.shard_map(
        functools.partial(per_device, mesh.shape["row"], mesh.shape["col"]),
        mesh=mesh,
        in_specs=(
            P(None, None, "row", "col"),
            P(),
            P(),
            P(None, ("row", "col")),
            P(None, ("row", "col")),
        ),
        out_specs=P(None, None, "row", "col"),
        check_vma=False,
    )
```

```python
import functools

import jax
import jax.numpy as jnp
from jax import lax
from jax.experimental import pallas as pl
from jax.experimental.pallas import tpu as pltpu
from jax.sharding import PartitionSpec as P

MESH = pl.DeviceIdType.MESH
F32 = jnp.float32
BF16 = jnp.bfloat16
COMPS = 3
GROUP = 4
RETURN_ORDER = (0, 1, 2, 4, 3, 7, 6, 5)


def return_order(n_z):
    return [p for p in RETURN_ORDER if p < n_z] + list(range(len(RETURN_ORDER), n_z))


def kernel(
    n_row, n_col,
    vel, dy_hbm, dz_hbm, force_hbm, cell_hbm,
    out,
    dy, dz, force, cell, vw, y_in, z_in, y_out, z_out, y_back, z_back, node_tile, node_z, node_sum, node_all, delta,
    load_sem, y_in_sem, z_in_sem, y_back_sem, z_back_sem, node_sem,
    y_in_send, z_in_send, y_back_send, z_back_send, node_send,
):
    r = lax.axis_index("row")
    c = lax.axis_index("col")
    ny, nz = vel.shape[2], vel.shape[3]
    planes = vel.shape[1] // n_col
    n_nodes = force_hbm.shape[1]

    barrier = pltpu.get_barrier_semaphore()

    n_z = n_row // GROUP
    for d in sorted(range(n_z), key=lambda d: -min(d, n_z - d)):
        for e in range(GROUP):
            if d or e:
                to = lax.rem(r // GROUP + d, n_z) * GROUP + lax.rem(r + e, GROUP)
                pl.semaphore_signal(barrier, inc=1, device_id={"row": to}, device_id_type=MESH)
    for d in range(1, n_col):
        pl.semaphore_signal(
            barrier, inc=1, device_id={"col": lax.rem(c + d, n_col)}, device_id_type=MESH
        )

    load_dy = pltpu.make_async_copy(dy_hbm, dy, load_sem.at[0])
    load_dz = pltpu.make_async_copy(dz_hbm, dz, load_sem.at[1])
    load_vw = pltpu.make_async_copy(vel.at[pl.ds(1, 2)], vw, load_sem.at[2])
    load_force = pltpu.make_async_copy(force_hbm, force, load_sem.at[3])
    load_cell = pltpu.make_async_copy(cell_hbm, cell, load_sem.at[4])
    load_force.start()
    load_cell.start()

    group = (n_row * n_nodes) // 128
    per_tile = n_row // group
    lane = lax.broadcasted_iota(jnp.int32, (COMPS, 128), 1)
    base = lax.rem(r, per_tile) * n_nodes
    load_force.wait()
    load_cell.wait()
    forces, cells = force[...], cell[...].astype(F32)
    spread_f = jnp.zeros((COMPS, 128), F32)
    spread_c = jnp.zeros((COMPS, 128), F32)
    for k in range(n_nodes):
        spread_f = jnp.where(lane == base + k, forces[:, k : k + 1], spread_f)
        spread_c = jnp.where(lane == base + k, cells[:, k : k + 1], spread_c)
    node_tile[...] = jnp.zeros_like(node_tile)
    node_tile[0:COMPS, :] = spread_f
    node_tile[4 : 4 + COMPS, :] = spread_c

    pl.semaphore_wait(barrier, n_row + n_col - 2)

    for k in range(COMPS):

        @pl.loop(1, n_row)
        def _(s):
            to = lax.rem(r + s, n_row)
            pltpu.make_async_remote_copy(
                src_ref=vel.at[k, to],
                dst_ref=y_in.at[k, pl.ds(pl.multiple_of(r * ny, ny), ny)],
                send_sem=y_in_send.at[k],
                recv_sem=y_in_sem.at[k],
                device_id={"row": to},
                device_id_type=MESH,
            ).start()

        @pl.loop(1, n_col)
        def _(s):
            to = lax.rem(c + s, n_col)
            pltpu.make_async_remote_copy(
                src_ref=vel.at[k, pl.ds(to * planes, planes)],
                dst_ref=z_in.at[k, c],
                send_sem=z_in_send.at[k],
                recv_sem=z_in_sem.at[k],
                device_id={"col": to},
                device_id_type=MESH,
            ).start()

        pltpu.make_async_copy(
            vel.at[k, r], y_in.at[k, pl.ds(pl.multiple_of(r * ny, ny), ny)], y_in_sem.at[k]
        ).start()
        pltpu.make_async_copy(
            vel.at[k, pl.ds(c * planes, planes)], z_in.at[k, c], z_in_sem.at[k]
        ).start()
        if k == 0:
            load_dy.start()
            load_dz.start()
            load_vw.start()

            for d in range(1, n_z):
                to_z = lax.rem(r // GROUP + d, n_z)
                pltpu.make_async_remote_copy(
                    src_ref=node_tile,
                    dst_ref=node_z.at[r // GROUP],
                    send_sem=node_send.at[0],
                    recv_sem=node_sem.at[0],
                    device_id={"row": to_z * GROUP + lax.rem(r, GROUP)},
                    device_id_type=MESH,
                ).start()

            pltpu.make_async_copy(node_tile, node_z.at[r // GROUP], node_sem.at[0]).start()

    load_dy.wait()
    load_dz.wait()
    def y_part(k):
        pltpu.make_async_copy(y_in.at[k], y_in.at[k], y_in_sem.at[k]).wait()
        lines = y_in[k].astype(BF16)
        rows = 256 if dy.shape[0] % 256 == 0 else dy.shape[0]
        for m in range(dy.shape[0] // rows):
            y_out[k, m * rows : (m + 1) * rows, :] = jnp.dot(
                dy[m * rows : (m + 1) * rows, :], lines, preferred_element_type=F32
            )

        def y_return(to):
            pltpu.make_async_remote_copy(
                src_ref=y_out.at[k, pl.ds(pl.multiple_of(to * ny, ny), ny)],
                dst_ref=y_back.at[k, r],
                send_sem=y_back_send.at[k],
                recv_sem=y_back_sem.at[k],
                device_id={"row": to},
                device_id_type=MESH,
            ).start()

        for to_z in return_order(n_row // GROUP):

            @pl.loop(0, GROUP)
            def _(s):
                to = to_z * GROUP + lax.rem(r + s, GROUP)

                @pl.when(to != r)
                def _():
                    y_return(to)

        pltpu.make_async_copy(
            y_out.at[k, pl.ds(pl.multiple_of(r * ny, ny), ny)], y_back.at[k, r], y_back_sem.at[k]
        ).start()

    def z_part(k):
        pltpu.make_async_copy(z_in.at[k], z_in.at[k], z_in_sem.at[k]).wait()
        lines = jnp.concatenate(
            [z_in[k, j].reshape(planes * ny, nz) for j in range(n_col)], axis=1
        ).astype(BF16)
        for j in range(n_col):
            z_out[k, j] = lax.dot_general(
                lines, dz[j * nz : (j + 1) * nz, :], (((1,), (1,)), ((), ())),
                preferred_element_type=F32,
            ).reshape(planes, ny, nz)

        @pl.loop(1, n_col)
        def _(s):
            to = lax.rem(c + s, n_col)
            pltpu.make_async_remote_copy(
                src_ref=z_out.at[k, to],
                dst_ref=z_back.at[k, pl.ds(c * planes, planes)],
                send_sem=z_back_send.at[k],
                recv_sem=z_back_sem.at[k],
                device_id={"col": to},
                device_id_type=MESH,
            ).start()

        pltpu.make_async_copy(
            z_out.at[k, c], z_back.at[k, pl.ds(c * planes, planes)], z_back_sem.at[k]
        ).start()

    y_part(0)
    z_part(0)
    pltpu.make_async_copy(node_z, node_z, node_sem.at[0]).wait()
    z_per_tile = per_tile // GROUP
    for g in range(group):
        total = node_z[g * z_per_tile]
        for j in range(1, z_per_tile):
            total = total + node_z[g * z_per_tile + j]
        node_sum[g] = total
    for d in range(1, GROUP):
        to_q = lax.rem(r + d, GROUP)
        pltpu.make_async_remote_copy(
            src_ref=node_sum,
            dst_ref=node_all.at[lax.rem(r, GROUP)],
            send_sem=node_send.at[1],
            recv_sem=node_sem.at[1],
            device_id={"row": r // GROUP * GROUP + to_q},
            device_id_type=MESH,
        ).start()
    pltpu.make_async_copy(node_sum, node_all.at[lax.rem(r, GROUP)], node_sem.at[1]).start()
    y_part(1)
    y_part(2)
    z_part(1)
    z_part(2)

    pltpu.make_async_copy(node_all, node_all, node_sem.at[1]).wait()
    tiles = []
    for g in range(group):
        total = node_all[0, g]
        for j in range(1, GROUP):
            total = total + node_all[j, g]
        tiles.append(total)
    nodes = jnp.concatenate(tiles, axis=1)
    count = 128 * group
    first_y = (r * ny).astype(F32)
    first_z = (c * nz).astype(F32)
    local_y = nodes[5:6, :] - first_y
    owned = (local_y >= 0.0) & (local_y < float(ny))
    key = jnp.where(owned, nodes[4:5, :] * float(ny) + local_y, -1.0)
    key_z = nodes[6:7, :] - first_z
    z_pos = lax.broadcasted_iota(jnp.int32, (nz, count), 0).astype(F32)
    hot_z = jnp.where(z_pos == key_z, 1.0, 0.0).astype(BF16)
    high = nodes.astype(BF16).astype(F32)
    rest = nodes - high
    mid = rest.astype(BF16).astype(F32)
    low = rest - mid
    rows = vel.shape[1] * ny
    step = 256 if rows % 256 == 0 else rows

    @pl.loop(0, rows // step)
    def _(m):
        pos = (lax.broadcasted_iota(jnp.int32, (step, count), 0) + m * step).astype(F32)
        hit = pos == key
        for k in range(COMPS):
            total = jnp.zeros((step, nz), F32)
            for part in (high, mid, low):
                pushed = jnp.where(hit, part[k : k + 1, :], 0.0).astype(BF16)
                total = total + lax.dot_general(
                    pushed, hot_z, (((1,), (1,)), ((), ())), preferred_element_type=F32
                )
            delta[k, pl.ds(pl.multiple_of(m * step, step), step), :] = total

    load_vw.wait()
    for k in range(COMPS):
        pltpu.make_async_copy(y_back.at[k], y_back.at[k], y_back_sem.at[k]).wait()
        pltpu.make_async_copy(z_back.at[k], z_back.at[k], z_back_sem.at[k]).wait()
        out[k] = delta[k].reshape(out.shape[1:]) - (vw[0] * y_back[k] + vw[1] * z_back[k])

    for k in range(COMPS):
        y_sent = y_in.at[k, pl.ds(0, (n_row - 1) * ny)]
        z_sent = z_in.at[k, pl.ds(0, n_col - 1)]
        pltpu.make_async_copy(y_sent, y_sent, y_in_send.at[k]).wait()
        pltpu.make_async_copy(z_sent, z_sent, z_in_send.at[k]).wait()
        pltpu.make_async_copy(y_sent, y_sent, y_back_send.at[k]).wait()
        pltpu.make_async_copy(z_sent, z_sent, z_back_send.at[k]).wait()
    z_sent = node_z.at[pl.ds(0, n_z - 1)]
    group_sent = node_all.at[pl.ds(0, GROUP - 1)]
    pltpu.make_async_copy(z_sent, z_sent, node_send.at[0]).wait()
    pltpu.make_async_copy(group_sent, group_sent, node_send.at[1]).wait()


def per_device(n_row, n_col, velocity, dy_op, dz_op, node_force, node_cell):
    _, n_x, ny, nz = velocity.shape
    planes = n_x // n_col
    node_tiles = n_row * node_force.shape[1] // 128
    dma = pltpu.SemaphoreType.DMA
    hbm = pl.BlockSpec(memory_space=pltpu.HBM)
    vmem = pl.BlockSpec(memory_space=pltpu.VMEM)
    return pl.pallas_call(
        functools.partial(kernel, n_row, n_col),
        out_shape=jax.ShapeDtypeStruct(velocity.shape, F32),
        in_specs=[hbm] * 5,
        out_specs=vmem,
        scratch_shapes=[
            pltpu.VMEM(dy_op.shape, BF16),
            pltpu.VMEM(dz_op.shape, BF16),
            pltpu.VMEM(node_force.shape, F32),
            pltpu.VMEM(node_cell.shape, jnp.int32),
            pltpu.VMEM((2, n_x, ny, nz), F32),
            pltpu.VMEM((COMPS, n_row * ny, nz), F32),
            pltpu.VMEM((COMPS, n_col, planes, ny, nz), F32),
            pltpu.VMEM((COMPS, n_row * ny, nz), F32),
            pltpu.VMEM((COMPS, n_col, planes, ny, nz), F32),
            pltpu.VMEM((COMPS, n_x, ny, nz), F32),
            pltpu.VMEM((COMPS, n_x, ny, nz), F32),
            pltpu.VMEM((8, 128), F32),
            pltpu.VMEM((n_row // GROUP, 8, 128), F32),
            pltpu.VMEM((node_tiles, 8, 128), F32),
            pltpu.VMEM((GROUP, node_tiles, 8, 128), F32),
            pltpu.VMEM((COMPS, n_x * ny, nz), F32),
            dma((5,)), dma((COMPS,)), dma((COMPS,)), dma((COMPS,)), dma((COMPS,)), dma((2,)),
            dma((COMPS,)), dma((COMPS,)), dma((COMPS,)), dma((COMPS,)), dma((2,)),
        ],
        compiler_params=pltpu.CompilerParams(
            collective_id=0, has_side_effects=True, vmem_limit_bytes=40 * 1024 * 1024
        ),
    )(*(
        pltpu.with_memory_space_constraint(x, pltpu.HBM)
        for x in (velocity, dy_op, dz_op, node_force, node_cell)
    ))


def solution(mesh):
    return jax.shard_map(
        functools.partial(per_device, mesh.shape["row"], mesh.shape["col"]),
        mesh=mesh,
        in_specs=(
            P(None, None, "row", "col"),
            P(),
            P(),
            P(None, ("row", "col")),
            P(None, ("row", "col")),
        ),
        out_specs=P(None, None, "row", "col"),
        check_vma=False,
    )
```

```python
import functools

import jax
import jax.numpy as jnp
from jax import lax
from jax.experimental import pallas as pl
from jax.experimental.pallas import tpu as pltpu
from jax.sharding import PartitionSpec as P

MESH = pl.DeviceIdType.MESH
F32 = jnp.float32
BF16 = jnp.bfloat16
COMPS = 3
PARTS = ((0, 1), (1, 2))
GROUP = 4
RETURN_ORDER = (0, 1, 2, 3, 4, 7, 6, 5)


def return_order(n_z):
    return [p for p in RETURN_ORDER if p < n_z] + list(range(len(RETURN_ORDER), n_z))


def kernel(
    n_row, n_col,
    vel, dy_hbm, dz_hbm, force_hbm, cell_hbm,
    out,
    dy, dz, force, cell, vw, y_in, z_in, y_out, z_out, y_back, z_back, node_tile, node_z, node_sum, node_all, delta,
    load_sem, y_in_sem, z_in_sem, y_back_sem, z_back_sem, node_sem,
    y_in_send, z_in_send, y_back_send, z_back_send, node_send,
):
    r = lax.axis_index("row")
    c = lax.axis_index("col")
    ny, nz = vel.shape[2], vel.shape[3]
    planes = vel.shape[1] // n_col
    n_nodes = force_hbm.shape[1]

    barrier = pltpu.get_barrier_semaphore()

    n_z = n_row // GROUP
    for d in sorted(range(n_z), key=lambda d: -min(d, n_z - d)):
        for e in range(GROUP):
            if d or e:
                to = lax.rem(r // GROUP + d, n_z) * GROUP + lax.rem(r + e, GROUP)
                pl.semaphore_signal(barrier, inc=1, device_id={"row": to}, device_id_type=MESH)
    for d in range(1, n_col):
        pl.semaphore_signal(
            barrier, inc=1, device_id={"col": lax.rem(c + d, n_col)}, device_id_type=MESH
        )

    load_dy = pltpu.make_async_copy(dy_hbm, dy, load_sem.at[0])
    load_dz = pltpu.make_async_copy(dz_hbm, dz, load_sem.at[1])
    load_vw = pltpu.make_async_copy(vel.at[pl.ds(1, 2)], vw, load_sem.at[2])
    load_force = pltpu.make_async_copy(force_hbm, force, load_sem.at[3])
    load_cell = pltpu.make_async_copy(cell_hbm, cell, load_sem.at[4])
    load_force.start()
    load_cell.start()

    group = (n_row * n_nodes) // 128
    per_tile = n_row // group
    lane = lax.broadcasted_iota(jnp.int32, (COMPS, 128), 1)
    base = lax.rem(r, per_tile) * n_nodes
    load_force.wait()
    load_cell.wait()
    forces, cells = force[...], cell[...].astype(F32)
    spread_f = jnp.zeros((COMPS, 128), F32)
    spread_c = jnp.zeros((COMPS, 128), F32)
    for k in range(n_nodes):
        spread_f = jnp.where(lane == base + k, forces[:, k : k + 1], spread_f)
        spread_c = jnp.where(lane == base + k, cells[:, k : k + 1], spread_c)
    node_tile[...] = jnp.zeros_like(node_tile)
    node_tile[0:COMPS, :] = spread_f
    node_tile[COMPS : 2 * COMPS, :] = spread_c

    pl.semaphore_wait(barrier, n_row + n_col - 2)

    for k in range(COMPS):
        if k < len(PARTS):
            part = pl.ds(*PARTS[k])
            own = y_in.at[part, pl.ds(pl.multiple_of(r * ny, ny), ny)]

            @pl.loop(1, n_row)
            def _(s):
                to = lax.rem(r + s, n_row)
                pltpu.make_async_remote_copy(
                    src_ref=vel.at[part, to],
                    dst_ref=own,
                    send_sem=y_in_send.at[k],
                    recv_sem=y_in_sem.at[k],
                    device_id={"row": to},
                    device_id_type=MESH,
                ).start()

            pltpu.make_async_copy(vel.at[part, r], own, y_in_sem.at[k]).start()

        @pl.loop(1, n_col)
        def _(s):
            to = lax.rem(c + s, n_col)
            pltpu.make_async_remote_copy(
                src_ref=vel.at[k, pl.ds(to * planes, planes)],
                dst_ref=z_in.at[k, c],
                send_sem=z_in_send.at[k],
                recv_sem=z_in_sem.at[k],
                device_id={"col": to},
                device_id_type=MESH,
            ).start()

        pltpu.make_async_copy(
            vel.at[k, pl.ds(c * planes, planes)], z_in.at[k, c], z_in_sem.at[k]
        ).start()
        if k == 0:
            load_dy.start()
            load_dz.start()
            load_vw.start()

            for d in range(1, n_z):
                to_z = lax.rem(r // GROUP + d, n_z)
                pltpu.make_async_remote_copy(
                    src_ref=node_tile,
                    dst_ref=node_z.at[r // GROUP],
                    send_sem=node_send.at[0],
                    recv_sem=node_sem.at[0],
                    device_id={"row": to_z * GROUP + lax.rem(r, GROUP)},
                    device_id_type=MESH,
                ).start()

            pltpu.make_async_copy(node_tile, node_z.at[r // GROUP], node_sem.at[0]).start()

    load_dy.wait()
    load_dz.wait()
    def y_part(k):
        first, n = PARTS[k]
        part = pl.ds(first, n)
        pltpu.make_async_copy(y_in.at[part], y_in.at[part], y_in_sem.at[k]).wait()
        lines = jnp.concatenate([y_in[first + i] for i in range(n)], axis=1).astype(BF16)
        rows = 256 if dy.shape[0] % 256 == 0 else dy.shape[0]
        for m in range(dy.shape[0] // rows):
            span = slice(m * rows, (m + 1) * rows)
            both = jnp.dot(dy[span, :], lines, preferred_element_type=F32)
            for i in range(n):
                y_out[first + i, span, :] = both[:, i * nz : (i + 1) * nz]

        def y_return(to):
            pltpu.make_async_remote_copy(
                src_ref=y_out.at[part, pl.ds(pl.multiple_of(to * ny, ny), ny)],
                dst_ref=y_back.at[part, r],
                send_sem=y_back_send.at[k],
                recv_sem=y_back_sem.at[k],
                device_id={"row": to},
                device_id_type=MESH,
            ).start()

        for to_z in return_order(n_row // GROUP):

            @pl.loop(0, GROUP)
            def _(s):
                to = to_z * GROUP + lax.rem(r + s, GROUP)

                @pl.when(to != r)
                def _():
                    y_return(to)

        pltpu.make_async_copy(
            y_out.at[part, pl.ds(pl.multiple_of(r * ny, ny), ny)], y_back.at[part, r],
            y_back_sem.at[k],
        ).start()

    def z_part(k):
        pltpu.make_async_copy(z_in.at[k], z_in.at[k], z_in_sem.at[k]).wait()
        lines = jnp.concatenate(
            [z_in[k, j].reshape(planes * ny, nz) for j in range(n_col)], axis=1
        ).astype(BF16)
        for j in range(n_col):
            z_out[k, j] = lax.dot_general(
                lines, dz[j * nz : (j + 1) * nz, :], (((1,), (1,)), ((), ())),
                preferred_element_type=F32,
            ).reshape(planes, ny, nz)

        @pl.loop(1, n_col)
        def _(s):
            to = lax.rem(c + s, n_col)
            pltpu.make_async_remote_copy(
                src_ref=z_out.at[k, to],
                dst_ref=z_back.at[k, pl.ds(c * planes, planes)],
                send_sem=z_back_send.at[k],
                recv_sem=z_back_sem.at[k],
                device_id={"col": to},
                device_id_type=MESH,
            ).start()

        pltpu.make_async_copy(
            z_out.at[k, c], z_back.at[k, pl.ds(c * planes, planes)], z_back_sem.at[k]
        ).start()

    y_part(0)
    z_part(0)
    pltpu.make_async_copy(node_z, node_z, node_sem.at[0]).wait()
    z_per_tile = per_tile // GROUP
    for g in range(group):
        total = node_z[g * z_per_tile]
        for j in range(1, z_per_tile):
            total = total + node_z[g * z_per_tile + j]
        node_sum[g] = total
    for d in range(1, GROUP):
        to_q = lax.rem(r + d, GROUP)
        pltpu.make_async_remote_copy(
            src_ref=node_sum,
            dst_ref=node_all.at[lax.rem(r, GROUP)],
            send_sem=node_send.at[1],
            recv_sem=node_sem.at[1],
            device_id={"row": r // GROUP * GROUP + to_q},
            device_id_type=MESH,
        ).start()
    pltpu.make_async_copy(node_sum, node_all.at[lax.rem(r, GROUP)], node_sem.at[1]).start()
    y_part(1)
    z_part(1)
    z_part(2)

    pltpu.make_async_copy(node_all, node_all, node_sem.at[1]).wait()
    tiles = []
    for g in range(group):
        total = node_all[0, g]
        for j in range(1, GROUP):
            total = total + node_all[j, g]
        tiles.append(total)
    nodes = jnp.concatenate(tiles, axis=1)
    count = 128 * group
    first_y = (r * ny).astype(F32)
    first_z = (c * nz).astype(F32)
    local_y = nodes[4:5, :] - first_y
    owned = (local_y >= 0.0) & (local_y < float(ny))
    key = jnp.where(owned, nodes[3:4, :] * float(ny) + local_y, -1.0)
    key_z = nodes[5:6, :] - first_z
    z_pos = lax.broadcasted_iota(jnp.int32, (nz, count), 0).astype(F32)
    hot_z = jnp.where(z_pos == key_z, 1.0, 0.0).astype(BF16)
    high = nodes.astype(BF16).astype(F32)
    rest = nodes - high
    mid = rest.astype(BF16).astype(F32)
    low = rest - mid
    rows = vel.shape[1] * ny
    step = 256 if rows % 256 == 0 else rows

    @pl.loop(0, rows // step)
    def _(m):
        pos = (lax.broadcasted_iota(jnp.int32, (step, count), 0) + m * step).astype(F32)
        hit = pos == key
        for k in range(COMPS):
            total = jnp.zeros((step, nz), F32)
            for part in (high, mid, low):
                pushed = jnp.where(hit, part[k : k + 1, :], 0.0).astype(BF16)
                total = total + lax.dot_general(
                    pushed, hot_z, (((1,), (1,)), ((), ())), preferred_element_type=F32
                )
            delta[k, pl.ds(pl.multiple_of(m * step, step), step), :] = total

    load_vw.wait()
    for k in range(COMPS):
        if k < len(PARTS):
            part = pl.ds(*PARTS[k])
            pltpu.make_async_copy(y_back.at[part], y_back.at[part], y_back_sem.at[k]).wait()
        out[k] = delta[k].reshape(out.shape[1:]) - vw[0] * y_back[k]
        pltpu.make_async_copy(z_back.at[k], z_back.at[k], z_back_sem.at[k]).wait()
        out[k] = out[k] - vw[1] * z_back[k]

    for k in range(COMPS):
        z_sent = z_in.at[k, pl.ds(0, n_col - 1)]
        pltpu.make_async_copy(z_sent, z_sent, z_in_send.at[k]).wait()
        pltpu.make_async_copy(z_sent, z_sent, z_back_send.at[k]).wait()
    for k in range(len(PARTS)):
        y_sent = y_in.at[pl.ds(*PARTS[k]), pl.ds(0, (n_row - 1) * ny)]
        pltpu.make_async_copy(y_sent, y_sent, y_in_send.at[k]).wait()
        pltpu.make_async_copy(y_sent, y_sent, y_back_send.at[k]).wait()
    z_sent = node_z.at[pl.ds(0, n_z - 1)]
    group_sent = node_all.at[pl.ds(0, GROUP - 1)]
    pltpu.make_async_copy(z_sent, z_sent, node_send.at[0]).wait()
    pltpu.make_async_copy(group_sent, group_sent, node_send.at[1]).wait()


def per_device(n_row, n_col, velocity, dy_op, dz_op, node_force, node_cell):
    _, n_x, ny, nz = velocity.shape
    planes = n_x // n_col
    node_tiles = n_row * node_force.shape[1] // 128
    dma = pltpu.SemaphoreType.DMA
    hbm = pl.BlockSpec(memory_space=pltpu.HBM)
    vmem = pl.BlockSpec(memory_space=pltpu.VMEM)
    return pl.pallas_call(
        functools.partial(kernel, n_row, n_col),
        out_shape=jax.ShapeDtypeStruct(velocity.shape, F32),
        in_specs=[hbm] * 5,
        out_specs=vmem,
        scratch_shapes=[
            pltpu.VMEM(dy_op.shape, BF16),
            pltpu.VMEM(dz_op.shape, BF16),
            pltpu.VMEM(node_force.shape, F32),
            pltpu.VMEM(node_cell.shape, jnp.int32),
            pltpu.VMEM((2, n_x, ny, nz), F32),
            pltpu.VMEM((COMPS, n_row * ny, nz), F32),
            pltpu.VMEM((COMPS, n_col, planes, ny, nz), F32),
            pltpu.VMEM((COMPS, n_row * ny, nz), F32),
            pltpu.VMEM((COMPS, n_col, planes, ny, nz), F32),
            pltpu.VMEM((COMPS, n_x, ny, nz), F32),
            pltpu.VMEM((COMPS, n_x, ny, nz), F32),
            pltpu.VMEM((8, 128), F32),
            pltpu.VMEM((n_row // GROUP, 8, 128), F32),
            pltpu.VMEM((node_tiles, 8, 128), F32),
            pltpu.VMEM((GROUP, node_tiles, 8, 128), F32),
            pltpu.VMEM((COMPS, n_x * ny, nz), F32),
            dma((5,)), dma((COMPS,)), dma((COMPS,)), dma((COMPS,)), dma((COMPS,)), dma((2,)),
            dma((COMPS,)), dma((COMPS,)), dma((COMPS,)), dma((COMPS,)), dma((2,)),
        ],
        compiler_params=pltpu.CompilerParams(
            collective_id=0, has_side_effects=True, vmem_limit_bytes=40 * 1024 * 1024
        ),
    )(*(
        pltpu.with_memory_space_constraint(x, pltpu.HBM)
        for x in (velocity, dy_op, dz_op, node_force, node_cell)
    ))


def solution(mesh):
    return jax.shard_map(
        functools.partial(per_device, mesh.shape["row"], mesh.shape["col"]),
        mesh=mesh,
        in_specs=(
            P(None, None, "row", "col"),
            P(),
            P(),
            P(None, ("row", "col")),
            P(None, ("row", "col")),
        ),
        out_specs=P(None, None, "row", "col"),
        check_vma=False,
    )
```

```python
import functools

import jax
import jax.numpy as jnp
from jax import lax
from jax.experimental import pallas as pl
from jax.experimental.pallas import tpu as pltpu
from jax.sharding import PartitionSpec as P

MESH = pl.DeviceIdType.MESH
F32 = jnp.float32
BF16 = jnp.bfloat16
COMPS = 3
GROUP = 4
RETURN_ORDER = (0, 1, 2, 3, 4, 7, 6, 5)


def return_order(n_z):
    return [p for p in RETURN_ORDER if p < n_z] + list(range(len(RETURN_ORDER), n_z))


def kernel(
    n_row, n_col,
    vel, dy_hbm, dz_hbm, force_hbm, cell_hbm,
    out,
    dy, dz, force, cell, vw, y_in, z_in, y_out, z_out, y_back, z_back, node_tile, node_z, node_sum, node_all, delta,
    load_sem, y_in_sem, z_in_sem, y_back_sem, z_back_sem, node_sem,
    y_in_send, z_in_send, y_back_send, z_back_send, node_send,
):
    r = lax.axis_index("row")
    c = lax.axis_index("col")
    ny, nz = vel.shape[2], vel.shape[3]
    planes = vel.shape[1] // n_col
    n_nodes = force_hbm.shape[1]

    barrier = pltpu.get_barrier_semaphore()

    n_z = n_row // GROUP
    for d in sorted(range(n_z), key=lambda d: -min(d, n_z - d)):
        for e in range(GROUP):
            if d or e:
                to = lax.rem(r // GROUP + d, n_z) * GROUP + lax.rem(r + e, GROUP)
                pl.semaphore_signal(barrier, inc=1, device_id={"row": to}, device_id_type=MESH)
    for d in range(1, n_col):
        pl.semaphore_signal(
            barrier, inc=1, device_id={"col": lax.rem(c + d, n_col)}, device_id_type=MESH
        )

    load_dy = pltpu.make_async_copy(dy_hbm, dy, load_sem.at[0])
    load_dz = pltpu.make_async_copy(dz_hbm, dz, load_sem.at[1])
    load_vw = pltpu.make_async_copy(vel.at[pl.ds(1, 2)], vw, load_sem.at[2])
    load_force = pltpu.make_async_copy(force_hbm, force, load_sem.at[3])
    load_cell = pltpu.make_async_copy(cell_hbm, cell, load_sem.at[4])
    load_force.start()
    load_cell.start()

    group = (n_row * n_nodes) // 128
    per_tile = n_row // group
    lane = lax.broadcasted_iota(jnp.int32, (COMPS, 128), 1)
    base = lax.rem(r, per_tile) * n_nodes
    load_force.wait()
    load_cell.wait()
    forces, cells = force[...], cell[...].astype(F32)
    spread_f = jnp.zeros((COMPS, 128), F32)
    spread_c = jnp.zeros((COMPS, 128), F32)
    for k in range(n_nodes):
        spread_f = jnp.where(lane == base + k, forces[:, k : k + 1], spread_f)
        spread_c = jnp.where(lane == base + k, cells[:, k : k + 1], spread_c)
    node_tile[...] = jnp.zeros_like(node_tile)
    node_tile[0:COMPS, :] = spread_f
    node_tile[COMPS : 2 * COMPS, :] = spread_c

    pl.semaphore_wait(barrier, n_row + n_col - 2)

    def row_forward(k):
        @pl.loop(1, n_row)
        def _(s):
            to = lax.rem(r + s, n_row)
            pltpu.make_async_remote_copy(
                src_ref=vel.at[k, to],
                dst_ref=y_in.at[k, pl.ds(pl.multiple_of(r * ny, ny), ny)],
                send_sem=y_in_send.at[k],
                recv_sem=y_in_sem.at[k],
                device_id={"row": to},
                device_id_type=MESH,
            ).start()

    def col_forward(k):
        @pl.loop(1, n_col)
        def _(s):
            to = lax.rem(c + s, n_col)
            pltpu.make_async_remote_copy(
                src_ref=vel.at[k, pl.ds(to * planes, planes)],
                dst_ref=z_in.at[k, c],
                send_sem=z_in_send.at[k],
                recv_sem=z_in_sem.at[k],
                device_id={"col": to},
                device_id_type=MESH,
            ).start()

    row_forward(0)
    col_forward(0)
    load_dy.start()
    load_dz.start()
    load_vw.start()

    for d in range(1, n_z):
        to_z = lax.rem(r // GROUP + d, n_z)
        pltpu.make_async_remote_copy(
            src_ref=node_tile,
            dst_ref=node_z.at[r // GROUP],
            send_sem=node_send.at[0],
            recv_sem=node_sem.at[0],
            device_id={"row": to_z * GROUP + lax.rem(r, GROUP)},
            device_id_type=MESH,
        ).start()

    pltpu.make_async_copy(node_tile, node_z.at[r // GROUP], node_sem.at[0]).start()

    row_forward(1)
    row_forward(2)
    col_forward(1)
    col_forward(2)

    for k in range(COMPS):
        pltpu.make_async_copy(
            vel.at[k, r], y_in.at[k, pl.ds(pl.multiple_of(r * ny, ny), ny)], y_in_sem.at[k]
        ).start()
        pltpu.make_async_copy(
            vel.at[k, pl.ds(c * planes, planes)], z_in.at[k, c], z_in_sem.at[k]
        ).start()

    load_dy.wait()
    load_dz.wait()
    def y_part(k):
        pltpu.make_async_copy(y_in.at[k], y_in.at[k], y_in_sem.at[k]).wait()
        lines = y_in[k].astype(BF16)
        rows = 256 if dy.shape[0] % 256 == 0 else dy.shape[0]
        for m in range(dy.shape[0] // rows):
            y_out[k, m * rows : (m + 1) * rows, :] = jnp.dot(
                dy[m * rows : (m + 1) * rows, :], lines, preferred_element_type=F32
            )

        def y_return(to):
            pltpu.make_async_remote_copy(
                src_ref=y_out.at[k, pl.ds(pl.multiple_of(to * ny, ny), ny)],
                dst_ref=y_back.at[k, r],
                send_sem=y_back_send.at[k],
                recv_sem=y_back_sem.at[k],
                device_id={"row": to},
                device_id_type=MESH,
            ).start()

        for to_z in return_order(n_row // GROUP):

            @pl.loop(0, GROUP)
            def _(s):
                to = to_z * GROUP + lax.rem(r + s, GROUP)

                @pl.when(to != r)
                def _():
                    y_return(to)

        pltpu.make_async_copy(
            y_out.at[k, pl.ds(pl.multiple_of(r * ny, ny), ny)], y_back.at[k, r], y_back_sem.at[k]
        ).start()

    def z_part(k):
        pltpu.make_async_copy(z_in.at[k], z_in.at[k], z_in_sem.at[k]).wait()
        lines = jnp.concatenate(
            [z_in[k, j].reshape(planes * ny, nz) for j in range(n_col)], axis=1
        ).astype(BF16)
        for j in range(n_col):
            z_out[k, j] = lax.dot_general(
                lines, dz[j * nz : (j + 1) * nz, :], (((1,), (1,)), ((), ())),
                preferred_element_type=F32,
            ).reshape(planes, ny, nz)

        @pl.loop(1, n_col)
        def _(s):
            to = lax.rem(c + s, n_col)
            pltpu.make_async_remote_copy(
                src_ref=z_out.at[k, to],
                dst_ref=z_back.at[k, pl.ds(c * planes, planes)],
                send_sem=z_back_send.at[k],
                recv_sem=z_back_sem.at[k],
                device_id={"col": to},
                device_id_type=MESH,
            ).start()

        pltpu.make_async_copy(
            z_out.at[k, c], z_back.at[k, pl.ds(c * planes, planes)], z_back_sem.at[k]
        ).start()

    y_part(0)
    z_part(0)
    pltpu.make_async_copy(node_z, node_z, node_sem.at[0]).wait()
    z_per_tile = per_tile // GROUP
    for g in range(group):
        total = node_z[g * z_per_tile]
        for j in range(1, z_per_tile):
            total = total + node_z[g * z_per_tile + j]
        node_sum[g] = total
    for d in range(1, GROUP):
        to_q = lax.rem(r + d, GROUP)
        pltpu.make_async_remote_copy(
            src_ref=node_sum,
            dst_ref=node_all.at[lax.rem(r, GROUP)],
            send_sem=node_send.at[1],
            recv_sem=node_sem.at[1],
            device_id={"row": r // GROUP * GROUP + to_q},
            device_id_type=MESH,
        ).start()
    pltpu.make_async_copy(node_sum, node_all.at[lax.rem(r, GROUP)], node_sem.at[1]).start()
    y_part(1)
    y_part(2)
    z_part(1)
    z_part(2)

    pltpu.make_async_copy(node_all, node_all, node_sem.at[1]).wait()
    tiles = []
    for g in range(group):
        total = node_all[0, g]
        for j in range(1, GROUP):
            total = total + node_all[j, g]
        tiles.append(total)
    nodes = jnp.concatenate(tiles, axis=1)
    count = 128 * group
    first_y = (r * ny).astype(F32)
    first_z = (c * nz).astype(F32)
    local_y = nodes[4:5, :] - first_y
    owned = (local_y >= 0.0) & (local_y < float(ny))
    key = jnp.where(owned, nodes[3:4, :] * float(ny) + local_y, -1.0)
    key_z = nodes[5:6, :] - first_z
    z_pos = lax.broadcasted_iota(jnp.int32, (nz, count), 0).astype(F32)
    hot_z = jnp.where(z_pos == key_z, 1.0, 0.0).astype(BF16)
    high = nodes.astype(BF16).astype(F32)
    rest = nodes - high
    mid = rest.astype(BF16).astype(F32)
    low = rest - mid
    rows = vel.shape[1] * ny
    step = 256 if rows % 256 == 0 else rows

    @pl.loop(0, rows // step)
    def _(m):
        pos = (lax.broadcasted_iota(jnp.int32, (step, count), 0) + m * step).astype(F32)
        hit = pos == key
        for k in range(COMPS):
            total = jnp.zeros((step, nz), F32)
            for part in (high, mid, low):
                pushed = jnp.where(hit, part[k : k + 1, :], 0.0).astype(BF16)
                total = total + lax.dot_general(
                    pushed, hot_z, (((1,), (1,)), ((), ())), preferred_element_type=F32
                )
            delta[k, pl.ds(pl.multiple_of(m * step, step), step), :] = total

    load_vw.wait()
    for k in range(COMPS):
        pltpu.make_async_copy(y_back.at[k], y_back.at[k], y_back_sem.at[k]).wait()
        out[k] = delta[k].reshape(out.shape[1:]) - vw[0] * y_back[k]
        pltpu.make_async_copy(z_back.at[k], z_back.at[k], z_back_sem.at[k]).wait()
        out[k] = out[k] - vw[1] * z_back[k]

    for k in range(COMPS):
        y_sent = y_in.at[k, pl.ds(0, (n_row - 1) * ny)]
        z_sent = z_in.at[k, pl.ds(0, n_col - 1)]
        pltpu.make_async_copy(y_sent, y_sent, y_in_send.at[k]).wait()
        pltpu.make_async_copy(z_sent, z_sent, z_in_send.at[k]).wait()
        pltpu.make_async_copy(y_sent, y_sent, y_back_send.at[k]).wait()
        pltpu.make_async_copy(z_sent, z_sent, z_back_send.at[k]).wait()
    z_sent = node_z.at[pl.ds(0, n_z - 1)]
    group_sent = node_all.at[pl.ds(0, GROUP - 1)]
    pltpu.make_async_copy(z_sent, z_sent, node_send.at[0]).wait()
    pltpu.make_async_copy(group_sent, group_sent, node_send.at[1]).wait()


def per_device(n_row, n_col, velocity, dy_op, dz_op, node_force, node_cell):
    _, n_x, ny, nz = velocity.shape
    planes = n_x // n_col
    node_tiles = n_row * node_force.shape[1] // 128
    dma = pltpu.SemaphoreType.DMA
    hbm = pl.BlockSpec(memory_space=pltpu.HBM)
    vmem = pl.BlockSpec(memory_space=pltpu.VMEM)
    return pl.pallas_call(
        functools.partial(kernel, n_row, n_col),
        out_shape=jax.ShapeDtypeStruct(velocity.shape, F32),
        in_specs=[hbm] * 5,
        out_specs=vmem,
        scratch_shapes=[
            pltpu.VMEM(dy_op.shape, BF16),
            pltpu.VMEM(dz_op.shape, BF16),
            pltpu.VMEM(node_force.shape, F32),
            pltpu.VMEM(node_cell.shape, jnp.int32),
            pltpu.VMEM((2, n_x, ny, nz), F32),
            pltpu.VMEM((COMPS, n_row * ny, nz), F32),
            pltpu.VMEM((COMPS, n_col, planes, ny, nz), F32),
            pltpu.VMEM((COMPS, n_row * ny, nz), F32),
            pltpu.VMEM((COMPS, n_col, planes, ny, nz), F32),
            pltpu.VMEM((COMPS, n_x, ny, nz), F32),
            pltpu.VMEM((COMPS, n_x, ny, nz), F32),
            pltpu.VMEM((8, 128), F32),
            pltpu.VMEM((n_row // GROUP, 8, 128), F32),
            pltpu.VMEM((node_tiles, 8, 128), F32),
            pltpu.VMEM((GROUP, node_tiles, 8, 128), F32),
            pltpu.VMEM((COMPS, n_x * ny, nz), F32),
            dma((5,)), dma((COMPS,)), dma((COMPS,)), dma((COMPS,)), dma((COMPS,)), dma((2,)),
            dma((COMPS,)), dma((COMPS,)), dma((COMPS,)), dma((COMPS,)), dma((2,)),
        ],
        compiler_params=pltpu.CompilerParams(
            collective_id=0, has_side_effects=True, vmem_limit_bytes=40 * 1024 * 1024
        ),
    )(*(
        pltpu.with_memory_space_constraint(x, pltpu.HBM)
        for x in (velocity, dy_op, dz_op, node_force, node_cell)
    ))


def solution(mesh):
    return jax.shard_map(
        functools.partial(per_device, mesh.shape["row"], mesh.shape["col"]),
        mesh=mesh,
        in_specs=(
            P(None, None, "row", "col"),
            P(),
            P(),
            P(None, ("row", "col")),
            P(None, ("row", "col")),
        ),
        out_specs=P(None, None, "row", "col"),
        check_vma=False,
    )
```
